1024 devices in a mesh: ctx: 128 (over z, y, core), head: 4 (over x_hi), batch: 2 (over x_lo).
Axes of the slice: x: 8 (x_hi: 4, x_lo: 2; x = x_hi * 2 + x_lo), y: 8, z: 8, core: 2. Of those that a mesh axis runs over, the one named last changes fastest.
Arguments:
- queries: bfloat16 [32768, 4096], P(('batch', 'ctx'), 'head'), parts along dimension 0, may hold values from -200 to 200
- key_rows: bfloat16 [32768, 1024], P(('batch', 'ctx'), 'head'), parts along dimension 0, may hold values from -7 to 7
- values: bfloat16 [32768, 1024], P(('batch', 'ctx'), 'head'), parts along dimension 0, may hold values from -6 to 6
- doc_lengths: int32 [128], P('batch'), parts along dimension 0, may hold values from 1 to 1920, 16384 in all
- out_weight: bfloat16 [4096, 4096], P('head'), may hold values from -0.125 to 0.125
Outputs:
- layer_out: bfloat16 [32768, 4096], P(('batch', 'ctx'), 'head'), parts along dimension 0
The draws below stay inside these ranges and needn't reach their ends.
There are 2 independent parts, one for each index of `batch`. The reference program is written for one: setup_inputs(seed, part) draws one part's arguments, and reference() takes and returns one part's arrays. A program takes and returns all parts, laid end to end along the dimension named above; an argument that names none is the same for every part. Nothing has to cross between parts.
Inputs may be any that keep to these rules, and one draw needn't show every extreme that they name: `doc_lengths`: the lengths sum to 16384, and the longest document has exactly 1920 tokens.
All inputs are finite; a program needn't handle non-finite values.
Results may differ from the reference program's by a relative error of at most 0.0052.
Values may be sent and summed in bfloat16 or wider, within the bound.
No kernel may reach another device: no remote copies, remote signals or barrier semaphores. Data moves between devices by JAX's collectives and lax.ppermute only.
A program may use at most 32 MiB of HBM per device.

```python
import math
import jax
import jax.numpy as jnp
import numpy as np
from jax import lax

D = 4096
HEADS = 32
KV_HEADS = 8
HEAD_DIM = 128
TOK_DEV = 128
SEQ = 16384
NDOCS = 64
REACH = 16
MAXDOC = 1920
N_CTX = 128


def pair_draw(key):
    folded = jax.random.fold_in(key, 7)
    key_main, key_query = jax.random.split(folded, 2)
    key_field = jnp.clip(jax.random.normal(key_main, (SEQ, KV_HEADS * HEAD_DIM), jnp.float32), -6.0, 6.0)
    query_field = jnp.clip(jax.random.normal(key_query, (SEQ, HEADS * HEAD_DIM), jnp.float32), -6.0, 6.0)
    return (query_field, key_field)


def draw_queries(key, part):
    return pair_draw(key)[0].astype(jnp.bfloat16)


def draw_key_rows(key, part):
    return pair_draw(key)[1].astype(jnp.bfloat16)


def strengthened(array, key, source, target, shards_of, factor):
    owner, partner = [(jnp.arange(array.shape[position]) // (array.shape[position] // shards_of)).reshape([-1 if axis == position else 1 for axis in range(array.ndim)]) for position in (source, target)]
    chosen = jax.random.permutation(key, shards_of)[partner]
    strong = (owner == chosen) | (owner == (partner + shards_of // 2) % shards_of)
    return jnp.where(strong, factor * array, array)


def shard_levels(stream_key, extent, cuts, smallest, top_value):
    def one(dim, parts):
        steps = jax.random.uniform(jax.random.fold_in(jax.random.fold_in(stream_key, 6), dim), (parts,), jnp.float32, smallest / len(cuts), top_value / len(cuts))
        return jnp.repeat(jnp.exp(steps), extent[dim] // parts).reshape((-1,) + (1,) * (len(extent) - dim - 1))

    level = one(*cuts[0])
    for cut in cuts[1:]:
        level = level * one(*cut)
    return level


def profile(count, total, bound, slope):
    portions = [(1 << 20) // math.isqrt(standing ** slope) + 1 for standing in range(2, count + 1)]
    surplus, given = total - bound - (count - 1), [1] * (count - 1)
    while surplus > 0:
        candidates = [i for i in range(count - 1) if given[i] < bound]
        whole, budget = sum([portions[i] for i in candidates]), surplus
        for i in candidates:
            addition = min(bound - given[i], max(1, budget * portions[i] // whole), surplus)
            given[i] = given[i] + addition
            surplus = surplus - addition
    return np.array([bound] + given)


def ragged(own_key, number_of, total, bound, skew):
    if number_of == 2:
        one = jax.random.randint(own_key, (), max(1, total - bound), min(bound, total - 1) + 1)
        return jnp.stack([one, total - one])
    tallies = jnp.asarray(profile(number_of, total, bound, skew), jnp.int32)
    pairs = (number_of - 1) // 2
    giver, sink = tallies[1:1 + 2 * pairs:2], tallies[2:2 + 2 * pairs:2]
    margin = jnp.minimum(giver - 1, bound - sink)
    moved = jax.random.randint(jax.random.fold_in(own_key, 1), (pairs,), 0, 1 << 20) % (margin + 1)
    tallies = tallies.at[1:1 + 2 * pairs:2].set(giver - moved).at[2:2 + 2 * pairs:2].set(sink + moved)
    return tallies[jax.random.permutation(jax.random.fold_in(own_key, 2), number_of)]


def normal_values(stream_key, extent, scale, most, cuts=(), kind=jnp.bfloat16):
    entries = jax.random.normal(stream_key, extent, jnp.float32) * scale
    if len(cuts) > 0:
        entries = shard_levels(stream_key, extent, cuts, -0.22, 0.18) * entries
    return jnp.clip(entries, min=-most, max=most).astype(kind)


def heavy_noise(rng, shape, deviation, bound, shards, heavy, kind=jnp.bfloat16):
    result = deviation * jax.random.normal(rng, shape, jnp.float32)
    if shards:
        result = result * shard_levels(rng, shape, shards, -0.22, 0.18)
    return jnp.clip(strengthened(result, jax.random.fold_in(rng, 3), *heavy), -bound, bound).astype(kind)


def setup_inputs(seed: int = 0, part: int = 0) -> dict:
    key_list = jax.random.split(jax.random.key(seed), 6)
    part_keys = jax.random.split(jax.random.fold_in(key_list[5], part), 6)
    return {
        "queries": draw_queries(jax.random.fold_in(jax.random.fold_in(key_list[5], part), 71), part),
        "key_rows": draw_key_rows(jax.random.fold_in(jax.random.fold_in(key_list[5], part), 71), part),
        "values": normal_values(part_keys[2], (SEQ, KV_HEADS * HEAD_DIM), 1.0, 6.0, ((0, 128), (1, 4))),
        "doc_lengths": ragged(part_keys[3], NDOCS, SEQ, MAXDOC, 2).astype(jnp.int32),
        "out_weight": heavy_noise(key_list[4], (HEADS * HEAD_DIM, D), (HEADS * HEAD_DIM) ** -0.5, 0.125, ((0, 4),), (0, 1, 4, 2.0)),
    }


def doc_ids(doc_ends, positions):
    return jnp.sum((doc_ends[None, :] <= positions[:, None]).astype(jnp.int32), axis=1).astype(jnp.int32)


def reference(queries, key_rows, values, doc_lengths, out_weight):
    group_size = HEADS // KV_HEADS
    window = (REACH - 1) * TOK_DEV
    kv_width = KV_HEADS * HEAD_DIM
    score_scale = HEAD_DIM ** -0.5
    doc_ends = jnp.cumsum(doc_lengths).astype(jnp.int32)
    positions = jnp.arange(SEQ, dtype=jnp.int32)
    query_docs_all = doc_ids(doc_ends, positions)
    pad_keys = jnp.concatenate([jnp.zeros((window, kv_width), jnp.bfloat16), key_rows], axis=0)
    pad_values = jnp.concatenate([jnp.zeros((window, kv_width), jnp.bfloat16), values], axis=0)
    key_docs_all = jnp.concatenate([jnp.full((window,), -1, jnp.int32), query_docs_all], axis=0)

    def one_block(block_index):
        first_row = (block_index * TOK_DEV).astype(jnp.int32)
        query_block = lax.dynamic_slice_in_dim(queries, first_row, TOK_DEV, 0).astype(jnp.float32)
        query_block = query_block.reshape(TOK_DEV, KV_HEADS, group_size, HEAD_DIM)
        key_block = lax.dynamic_slice_in_dim(pad_keys, first_row, window + TOK_DEV, 0).astype(jnp.float32)
        key_block = key_block.reshape(window + TOK_DEV, KV_HEADS, HEAD_DIM)
        value_block = lax.dynamic_slice_in_dim(pad_values, first_row, window + TOK_DEV, 0).astype(jnp.float32)
        value_block = value_block.reshape(window + TOK_DEV, KV_HEADS, HEAD_DIM)
        query_pos = first_row + jnp.arange(TOK_DEV, dtype=jnp.int32)
        key_pos = first_row - window + jnp.arange(window + TOK_DEV, dtype=jnp.int32)
        query_docs = lax.dynamic_slice_in_dim(query_docs_all, first_row, TOK_DEV, 0)
        key_docs = lax.dynamic_slice_in_dim(key_docs_all, first_row, window + TOK_DEV, 0)
        allowed = (key_docs[None, :] == query_docs[:, None]) & (key_pos[None, :] <= query_pos[:, None])
        scores = jnp.einsum("tkgd,skd->kgts", query_block, key_block) * score_scale
        scores = jnp.where(allowed[None, None], scores, -1e30)
        row_peak = jnp.max(scores, axis=3, keepdims=True)
        weights = jnp.exp(scores - row_peak)
        row_total = jnp.sum(weights, axis=3, keepdims=True)
        rounded = lax.optimization_barrier(weights.astype(jnp.bfloat16)).astype(jnp.float32)
        mixed_out = jnp.einsum("kgts,skd->tkgd", rounded, value_block)
        mixed_out = mixed_out / jnp.transpose(row_total, (2, 0, 1, 3))
        return mixed_out.astype(jnp.bfloat16).reshape(TOK_DEV, HEADS * HEAD_DIM)

    attended = lax.map(one_block, jnp.arange(N_CTX, dtype=jnp.int32)).reshape(SEQ, HEADS * HEAD_DIM)
    return jnp.dot(attended, out_weight, preferred_element_type=jnp.float32).astype(jnp.bfloat16)
```

```python
import jax
import jax.numpy as jnp
from jax import lax
from jax.sharding import PartitionSpec as P

HEADS = 32
KV_HEADS = 8
HEAD_DIM = 128


def chip_shift(value, chips, swap_core=False):
    devices = lax.axis_size("ctx")
    pairs = []
    for index in range(devices):
        target = (index + 2 * chips) % devices
        pairs.append((index, target ^ 1 if swap_core else target))
    return lax.ppermute(value, "ctx", pairs)


def per_device(queries, key_rows, values, doc_lengths, out_weight):
    my_index = lax.axis_index("ctx")
    head_index = lax.axis_index("head")
    head_devs = lax.axis_size("head")
    tok_rows = queries.shape[0]
    kv_width = key_rows.shape[1]
    local_heads = kv_width // HEAD_DIM
    group_size = HEADS // KV_HEADS
    score_scale = HEAD_DIM ** (-0.5)
    chip, core = my_index // 2, my_index % 2

    own = jnp.concatenate([key_rows, values], axis=1)
    back1 = chip_shift(own, 1)
    back7 = chip_shift(own, 7)
    back2 = chip_shift(back1, 1)
    back6 = chip_shift(back7, -1)
    back3 = chip_shift(back2, 1)
    back5 = chip_shift(back6, -1)
    back4 = chip_shift(back3, 1)
    back8 = chip_shift(own, 8, swap_core=True)
    local = jnp.concatenate([back7, back6, back5, back4, back3, back2, back1, own], axis=0)
    other = chip_shift(local, 0, swap_core=True)
    held = jnp.concatenate([back8, local, other], axis=0)

    rows = jnp.arange(tok_rows, dtype=jnp.int32)
    first = jnp.concatenate(
        [
            jnp.stack([(2 * (chip - 8) + 1 - core)]),
            2 * (chip - 7 + jnp.arange(8, dtype=jnp.int32)) + core,
            2 * (chip - 7 + jnp.arange(8, dtype=jnp.int32)) + 1 - core,
        ]
    )
    key_pos = (first[:, None] * tok_rows + rows[None, :]).reshape(-1)
    query_pos = my_index * tok_rows + rows
    doc_ends = jnp.cumsum(doc_lengths)
    doc_start = jnp.max(
        jnp.where(doc_ends[None, :] <= query_pos[:, None], doc_ends[None, :], 0), axis=1
    )
    allowed = (key_pos[None, :] >= doc_start[:, None]) & (key_pos[None, :] <= query_pos[:, None])
    pieces = []
    for pair in range(local_heads):
        query_block = queries[:, pair * group_size * HEAD_DIM : (pair + 1) * group_size * HEAD_DIM]
        query_block = query_block.reshape(tok_rows, group_size, HEAD_DIM)
        key_block = held[:, pair * HEAD_DIM : (pair + 1) * HEAD_DIM]
        value_block = held[:, kv_width + pair * HEAD_DIM : kv_width + (pair + 1) * HEAD_DIM]
        scores = (
            jnp.einsum("tgd,sd->gts", query_block, key_block, preferred_element_type=jnp.float32)
            * score_scale
        )
        scores = jnp.where(allowed[None], scores, -1e30)
        row_peak = jnp.max(scores, axis=2, keepdims=True)
        weights = jnp.exp(scores - row_peak)
        row_total = jnp.sum(weights, axis=2, keepdims=True)
        mixed_out = jnp.einsum(
            "gts,sd->gtd",
            weights.astype(jnp.bfloat16),
            value_block,
            preferred_element_type=jnp.float32,
        )
        mixed_out = mixed_out / row_total
        pieces.append(
            jnp.transpose(mixed_out, (1, 0, 2))
            .astype(jnp.bfloat16)
            .reshape(tok_rows, group_size * HEAD_DIM)
        )
    attended = jnp.concatenate(pieces, axis=1)
    width = out_weight.shape[1] // head_devs
    partial_out = jnp.dot(attended, out_weight, preferred_element_type=jnp.float32)

    def part(ahead):
        return lax.dynamic_slice_in_dim(
            partial_out, lax.rem(head_index + ahead, head_devs) * width, width, 1
        )

    total = part(0)
    for ahead in (2, 1, 3):
        got = lax.ppermute(
            part(ahead).astype(jnp.bfloat16),
            "head",
            [(i, (i + ahead) % head_devs) for i in range(head_devs)],
        )
        total = total + got.astype(jnp.float32)
    return total.astype(jnp.bfloat16)


def solution(mesh):
    return jax.shard_map(
        per_device,
        mesh=mesh,
        in_specs=(
            P(("batch", "ctx"), "head"),
            P(("batch", "ctx"), "head"),
            P(("batch", "ctx"), "head"),
            P("batch"),
            P("head", None),
        ),
        out_specs=P(("batch", "ctx"), "head"),
        check_vma=False,
    )
```

```python
import math

import jax
import jax.numpy as jnp
from jax import lax
from jax.experimental import pallas as pl
from jax.experimental.pallas import tpu as pltpu
from jax.sharding import PartitionSpec as P


HEADS = 32
KV_HEADS = 8
HEAD_DIM = 128
GROUP = HEADS // KV_HEADS
ROWS = 128
FAR = 1e30
BACK = 7
EXP_SCALE = HEAD_DIM ** (-0.5) * math.log2(math.e)


def chip_send(value, chips, targets):
    pairs = []
    for target in targets:
        if 0 <= target - chips < lax.axis_size("ctx") // 2:
            pairs += [(2 * (target - chips) + core, 2 * target + core) for core in range(2)]
    return lax.ppermute(value, "ctx", pairs)


def gather_blocks(own):
    chips = lax.axis_size("ctx") // 2
    back = {}
    back[1] = chip_send(own, 1, range(1, chips))
    back[7] = chip_send(own, 7, range(7, chips))
    for step in range(2, 5):
        back[step] = chip_send(back[step - 1], 1, range(step, chips))
        far = 8 - step
        if far > 4:
            relayed = chip_send(back[far + 1], -1, range(far, chips - step + 1))
            direct = chip_send(own, far, range(chips - step + 1, chips))
            back[far] = relayed + direct
    return back


def head_swap(value, stage):
    heads = lax.axis_size("head")
    pairs = []
    for index in range(lax.axis_size("ctx")):
        for head in range(heads):
            partner = head ^ 1 if (stage + index) % 2 == 0 else heads - 1 - head
            pairs.append((index * heads + head, index * heads + partner))
    return lax.ppermute(value, ("ctx", "head"), pairs)


def masked_bias(first, start_ref, query_first):
    lane = lax.broadcasted_iota(jnp.int32, (ROWS, ROWS), 1)
    row = lax.broadcasted_iota(jnp.int32, (ROWS, ROWS), 0)
    key_pos = lane + first
    keep = (key_pos >= start_ref[...]) & (key_pos <= row + query_first)
    return jnp.where(keep, 0.0, -FAR).astype(jnp.float32)


def stacked_queries(q_ref, pair):
    return jnp.concatenate(
        [
            q_ref[:, (pair * GROUP + h) * HEAD_DIM : (pair * GROUP + h + 1) * HEAD_DIM]
            for h in range(GROUP)
        ],
        axis=0,
    )


def biased_scores(q_ref, keys, bias, pair):
    scores = lax.dot_general(
        stacked_queries(q_ref, pair),
        keys,
        (((1,), (1,)), ((), ())),
        preferred_element_type=jnp.float32,
    )
    count = keys.shape[0]
    return (scores.reshape(GROUP, ROWS, count) + bias[None]).reshape(GROUP * ROWS, count)


def document_starts(length_ref, query_first):
    query_pos = lax.broadcasted_iota(jnp.int32, (8, ROWS), 1) + query_first
    starts = jnp.zeros_like(query_pos)
    end = jnp.int32(0)
    for i in range(length_ref.shape[0]):
        end = end + length_ref[i]
        starts = jnp.where(query_pos >= end, end, starts)
    return jnp.broadcast_to(starts[:1], (ROWS, ROWS)).T


def local_kernel(first_ref, length_ref, q_hbm, w_hbm, *refs):
    blocks, (peak_ref, total_ref, mixed_ref, start_ref, q_ref, w_ref, sems) = refs[:-7], refs[-7:]
    fetch_q = pltpu.make_async_copy(q_hbm, q_ref, sems.at[0])
    fetch_w = pltpu.make_async_copy(w_hbm.at[: w_ref.shape[0]], w_ref, sems.at[1])
    fetch_q.start()
    fetch_w.start()
    start_ref[...] = document_starts(length_ref, first_ref[len(blocks)])
    kv_width = blocks[0].shape[1] // 2
    bias = jnp.concatenate(
        [masked_bias(first_ref[i], start_ref, first_ref[len(blocks)]) for i in range(len(blocks))],
        axis=1,
    )
    fetch_q.wait()
    for pair in range(kv_width // HEAD_DIM):
        low, high = pair * HEAD_DIM, (pair + 1) * HEAD_DIM
        keys = jnp.concatenate([b[:, low:high] for b in blocks], axis=0)
        vals = jnp.concatenate([b[:, kv_width + low : kv_width + high] for b in blocks], axis=0)
        scores = biased_scores(q_ref, keys, bias, pair)
        peak = jnp.max(scores, axis=1, keepdims=True)
        weights = jnp.exp2((scores - peak) * EXP_SCALE)
        rows = slice(pair * GROUP * ROWS, (pair + 1) * GROUP * ROWS)
        wide = (GROUP * ROWS, HEAD_DIM)
        peak_ref[rows, :] = jnp.broadcast_to(peak, wide)
        total_ref[rows, :] = jnp.broadcast_to(jnp.sum(weights, axis=1, keepdims=True), wide)
        mixed_ref[rows, :] = jnp.dot(
            weights.astype(jnp.bfloat16), vals, preferred_element_type=jnp.float32
        )
    fetch_w.wait()


def project(attended, weights, column):
    rows, width = weights[0].shape[0], ROWS * GROUP * 2
    at = pl.multiple_of(column * width, width)
    return sum(
        jnp.dot(
            attended[:, i * rows : (i + 1) * rows],
            half[:, pl.ds(at, width)],
            preferred_element_type=jnp.float32,
        )
        for i, half in enumerate(weights)
    )


def rest_kernel(
    first_ref,
    w_hbm,
    other_ref,
    peak_ref,
    total_ref,
    mixed_ref,
    start_ref,
    q_ref,
    w_ref,
    *refs,
):
    outs, (attended_ref, w_rest_ref, sem) = refs[:-3], refs[-3:]
    fetch_w = pltpu.make_async_copy(w_hbm.at[w_ref.shape[0] :], w_rest_ref, sem)
    fetch_w.start()
    kv_width = other_ref.shape[1] // 2
    blocks = other_ref.shape[0] // ROWS
    bias = jnp.concatenate(
        [masked_bias(first_ref[i], start_ref, first_ref[blocks]) for i in range(blocks)], axis=1
    )
    for pair in range(kv_width // HEAD_DIM):
        low, high = pair * HEAD_DIM, (pair + 1) * HEAD_DIM
        scores = biased_scores(q_ref, other_ref[:, low:high], bias, pair)
        rows = slice(pair * GROUP * ROWS, (pair + 1) * GROUP * ROWS)
        old_peak = peak_ref[rows, :]
        peak = jnp.maximum(old_peak, jnp.max(scores, axis=1, keepdims=True))
        weights = jnp.exp2((scores - peak[:, :1]) * EXP_SCALE)
        keep = jnp.exp2((old_peak - peak) * EXP_SCALE)
        total = total_ref[rows, :] * keep + jnp.sum(weights, axis=1, keepdims=True)
        mixed = mixed_ref[rows, :] * keep + jnp.dot(
            weights.astype(jnp.bfloat16),
            other_ref[:, kv_width + low : kv_width + high],
            preferred_element_type=jnp.float32,
        )
        mixed = (mixed / total).astype(jnp.bfloat16)
        for h in range(GROUP):
            at = (pair * GROUP + h) * HEAD_DIM
            attended_ref[:, at : at + HEAD_DIM] = mixed[h * ROWS : (h + 1) * ROWS]
    fetch_w.wait()
    for i, out in enumerate(outs):
        part = project(attended_ref[...], (w_ref, w_rest_ref), first_ref[blocks + 1 + i])
        out[...] = part.astype(out.dtype)


def vmem(count):
    return [pl.BlockSpec(memory_space=pltpu.VMEM)] * count


def join_kernel(*refs):
    blocks, (first_ref, out_ref, first_out) = refs[:-3], refs[-3:]
    for i, block in enumerate(blocks):
        out_ref[i * ROWS : (i + 1) * ROWS, :] = block[...]
    first_out[...] = first_ref[...]


def join(blocks, cross):
    shape = (len(blocks) * ROWS, blocks[0].shape[1])
    return pl.pallas_call(
        join_kernel,
        out_shape=(
            jax.ShapeDtypeStruct(shape, blocks[0].dtype),
            jax.ShapeDtypeStruct(cross.shape, cross.dtype),
        ),
        in_specs=vmem(len(blocks) + 1),
        out_specs=tuple(vmem(2)),
        compiler_params=pltpu.CompilerParams(vmem_limit_bytes=4 * 2**20),
        name="join",
    )(*blocks, cross)


def half_weight(out_weight):
    rows, columns = out_weight.shape
    return jax.ShapeDtypeStruct((rows // 2, columns), out_weight.dtype)


def attend_local(firsts, doc_lengths, queries, out_weight, blocks):
    rows = queries.shape[0] * queries.shape[1] // HEAD_DIM
    state = jax.ShapeDtypeStruct((rows, HEAD_DIM), jnp.float32)
    keys = ROWS * len(blocks)
    return pl.pallas_call(
        local_kernel,
        out_shape=(state,) * 3
        + (
            jax.ShapeDtypeStruct((ROWS, ROWS), jnp.int32),
            jax.ShapeDtypeStruct(queries.shape, queries.dtype),
            half_weight(out_weight),
        ),
        in_specs=[pl.BlockSpec(memory_space=pltpu.SMEM)] * 2
        + [pl.BlockSpec(memory_space=pltpu.HBM)] * 2
        + vmem(len(blocks)),
        out_specs=tuple(vmem(6)),
        scratch_shapes=[pltpu.SemaphoreType.DMA((2,))],
        compiler_params=pltpu.CompilerParams(vmem_limit_bytes=16 * 2**20),
        cost_estimate=pl.CostEstimate(
            flops=4 * rows * keys * HEAD_DIM,
            bytes_accessed=4 * rows * keys,
            transcendentals=rows * keys,
        ),
        name="attend_local",
    )(firsts, doc_lengths, queries, out_weight, *blocks)


def attend_rest(firsts, out_weight, other, state, width):
    queries = state[-2]
    rows = queries.shape[0] * queries.shape[1] // HEAD_DIM
    keys = other.shape[0]
    half = half_weight(out_weight)
    kinds = (jnp.bfloat16, jnp.bfloat16, jnp.float32, jnp.float32)
    return pl.pallas_call(
        rest_kernel,
        out_shape=tuple(jax.ShapeDtypeStruct((queries.shape[0], width), k) for k in kinds),
        in_specs=[
            pl.BlockSpec(memory_space=pltpu.SMEM),
            pl.BlockSpec(memory_space=pltpu.HBM),
        ]
        + vmem(1 + len(state)),
        out_specs=tuple(vmem(4)),
        scratch_shapes=[
            pltpu.VMEM(queries.shape, jnp.bfloat16),
            pltpu.VMEM(half.shape, half.dtype),
            pltpu.SemaphoreType.DMA,
        ],
        compiler_params=pltpu.CompilerParams(vmem_limit_bytes=20 * 2**20),
        cost_estimate=pl.CostEstimate(
            flops=4 * rows * keys * HEAD_DIM + 8 * queries.size * width,
            bytes_accessed=4 * rows * keys + out_weight.size,
            transcendentals=rows * keys,
        ),
        name="attend_rest",
    )(firsts, out_weight, other, *state)


def layer(queries, key_rows, values, doc_lengths, out_weight):
    my_index = lax.axis_index("ctx")
    head = lax.axis_index("head")
    heads = lax.axis_size("head")
    chips = lax.axis_size("ctx") // 2
    chip, core = my_index // 2, my_index % 2

    kv_width = key_rows.shape[1]
    zero = jnp.zeros((), key_rows.dtype)
    own = lax.pad(key_rows, zero, ((0, 0, 0), (0, kv_width, 0))) + lax.pad(
        values, zero, ((0, 0, 0), (kv_width, 0, 0))
    )
    own = lax.optimization_barrier(own)
    cross = lax.ppermute(own, "ctx", [(2 * c - 15, 2 * c) for c in range(8, chips)])
    back = gather_blocks(own)
    blocks = [back[i] for i in range(BACK, 0, -1)] + [own]
    joined, cross = join(blocks, cross)
    blocks = blocks + [cross]
    other = lax.ppermute(joined, "ctx", [(i, i ^ 1) for i in range(2 * chips)])

    query_first = my_index * ROWS
    ahead = jnp.arange(BACK + 1, dtype=jnp.int32) - BACK + chip
    cross_first = jnp.where(core == 0, 2 * ROWS * (chip - 8) + ROWS, -ROWS)
    local_first = jnp.concatenate(
        [2 * ROWS * ahead + ROWS * core, jnp.stack([cross_first, query_first])]
    )
    doc_lengths = pltpu.with_memory_space_constraint(doc_lengths, pltpu.HBM)
    queries = pltpu.with_memory_space_constraint(queries, pltpu.HBM)
    out_weight = pltpu.with_memory_space_constraint(out_weight, pltpu.HBM)
    near, across = head ^ 1, heads - 1 - head
    first_mate = jnp.where(core == 0, near, across)
    second_mate = jnp.where(core == 0, across, near)
    rest_first = jnp.concatenate(
        [2 * ROWS * ahead + ROWS * (1 - core), jnp.stack([query_first, head ^ 2, first_mate, second_mate, head])]
    )
    width = out_weight.shape[1] // heads

    state = attend_local(local_first, doc_lengths, queries, out_weight, blocks)
    far_part, mate_part, second_part, own_part = attend_rest(
        rest_first, out_weight, other, state, width
    )
    far_got = head_swap(far_part, 0)
    mate_got = head_swap(mate_part, 0)
    passed = (second_part + far_got.astype(jnp.float32)).astype(jnp.bfloat16)
    last_got = head_swap(passed, 1)
    return (own_part + mate_got.astype(jnp.float32) + last_got.astype(jnp.float32)).astype(
        jnp.bfloat16
    )


def solution(mesh):
    return jax.shard_map(
        layer,
        mesh=mesh,
        in_specs=(
            P(("batch", "ctx"), "head"),
            P(("batch", "ctx"), "head"),
            P(("batch", "ctx"), "head"),
            P("batch"),
            P("head", None),
        ),
        out_specs=P(("batch", "ctx"), "head"),
        check_vma=False,
    )
```

```python
import math

import jax
import jax.numpy as jnp
from jax import lax
from jax.experimental import pallas as pl
from jax.experimental.pallas import tpu as pltpu
from jax.sharding import PartitionSpec as P


HEADS = 32
KV_HEADS = 8
HEAD_DIM = 128
GROUP = HEADS // KV_HEADS
ROWS = 128
FAR = 1e30
BACK = 7
EXP_SCALE = HEAD_DIM ** (-0.5) * math.log2(math.e)


def chip_send(value, chips, targets):
    pairs = []
    for target in targets:
        if 0 <= target - chips < lax.axis_size("ctx") // 2:
            pairs += [(2 * (target - chips) + core, 2 * target + core) for core in range(2)]
    return lax.ppermute(value, "ctx", pairs)


def gather_blocks(own):
    chips = lax.axis_size("ctx") // 2
    back = {}
    back[1] = chip_send(own, 1, range(1, chips))
    cross = lax.ppermute(own, "ctx", [(2 * c - 15, 2 * c) for c in range(8, chips)])
    back[7] = chip_send(own, 7, range(7, chips))
    back[2] = chip_send(back[1], 1, range(2, chips))
    relayed = chip_send(back[7], -1, range(6, chips - 1))
    back[6] = relayed + chip_send(own, 6, range(chips - 1, chips))
    back[3] = chip_send(back[2], 1, range(3, chips))
    back[4] = chip_send(back[2], 2, range(4, chips))
    relayed = chip_send(back[6], -1, range(5, chips - 2))
    back[5] = relayed + chip_send(own, 5, range(chips - 2, chips))
    return back, cross


def head_swap(value, stage):
    heads = lax.axis_size("head")
    pairs = []
    for index in range(lax.axis_size("ctx")):
        for head in range(heads):
            partner = head ^ 1 if (stage + index) % 2 == 0 else heads - 1 - head
            pairs.append((index * heads + head, index * heads + partner))
    return lax.ppermute(value, ("ctx", "head"), pairs)


def masked_bias(first, start_ref, query_first):
    lane = lax.broadcasted_iota(jnp.int32, (ROWS, ROWS), 1)
    row = lax.broadcasted_iota(jnp.int32, (ROWS, ROWS), 0)
    key_pos = lane + first
    keep = (key_pos >= start_ref[...]) & (key_pos <= row + query_first)
    return jnp.where(keep, 0.0, -FAR).astype(jnp.float32)


def stacked_queries(q_ref, pair):
    return jnp.concatenate(
        [
            q_ref[:, (pair * GROUP + h) * HEAD_DIM : (pair * GROUP + h + 1) * HEAD_DIM]
            for h in range(GROUP)
        ],
        axis=0,
    )


def biased_scores(q_ref, keys, bias, pair):
    scores = lax.dot_general(
        stacked_queries(q_ref, pair),
        keys,
        (((1,), (1,)), ((), ())),
        preferred_element_type=jnp.float32,
    )
    count = keys.shape[0]
    return (scores.reshape(GROUP, ROWS, count) + bias[None]).reshape(GROUP * ROWS, count)


def document_starts(length_ref, query_first):
    query_pos = lax.broadcasted_iota(jnp.int32, (8, ROWS), 1) + query_first
    starts = jnp.zeros_like(query_pos)
    end = jnp.int32(0)
    for i in range(length_ref.shape[0]):
        end = end + length_ref[i]
        starts = jnp.where(query_pos >= end, end, starts)
    return jnp.broadcast_to(starts[:1], (ROWS, ROWS)).T


def local_kernel(first_ref, length_ref, q_hbm, w_hbm, *refs):
    blocks, (peak_ref, total_ref, mixed_ref, start_ref, q_ref, w_ref, sems) = refs[:-7], refs[-7:]
    fetch_q = pltpu.make_async_copy(q_hbm, q_ref, sems.at[0])
    fetch_w = pltpu.make_async_copy(w_hbm.at[: w_ref.shape[0]], w_ref, sems.at[1])
    fetch_q.start()
    fetch_w.start()
    start_ref[...] = document_starts(length_ref, first_ref[len(blocks)])
    kv_width = blocks[0].shape[1] // 2
    bias = jnp.concatenate(
        [masked_bias(first_ref[i], start_ref, first_ref[len(blocks)]) for i in range(len(blocks))],
        axis=1,
    )
    fetch_q.wait()
    for pair in range(kv_width // HEAD_DIM):
        low, high = pair * HEAD_DIM, (pair + 1) * HEAD_DIM
        keys = jnp.concatenate([b[:, low:high] for b in blocks], axis=0)
        vals = jnp.concatenate([b[:, kv_width + low : kv_width + high] for b in blocks], axis=0)
        scores = biased_scores(q_ref, keys, bias, pair)
        peak = jnp.max(scores, axis=1, keepdims=True)
        weights = jnp.exp2((scores - peak) * EXP_SCALE)
        rows = slice(pair * GROUP * ROWS, (pair + 1) * GROUP * ROWS)
        wide = (GROUP * ROWS, HEAD_DIM)
        peak_ref[rows, :] = jnp.broadcast_to(peak, wide)
        total_ref[rows, :] = jnp.broadcast_to(jnp.sum(weights, axis=1, keepdims=True), wide)
        mixed_ref[rows, :] = jnp.dot(
            weights.astype(jnp.bfloat16), vals, preferred_element_type=jnp.float32
        )
    fetch_w.wait()


def project(attended, weights, column):
    rows, width = weights[0].shape[0], ROWS * GROUP * 2
    at = pl.multiple_of(column * width, width)
    return sum(
        jnp.dot(
            attended[:, i * rows : (i + 1) * rows],
            half[:, pl.ds(at, width)],
            preferred_element_type=jnp.float32,
        )
        for i, half in enumerate(weights)
    )


def rest_kernel(
    first_ref,
    w_hbm,
    other_ref,
    peak_ref,
    total_ref,
    mixed_ref,
    start_ref,
    q_ref,
    w_ref,
    *refs,
):
    outs, (attended_ref, w_rest_ref, sem) = refs[:-3], refs[-3:]
    fetch_w = pltpu.make_async_copy(w_hbm.at[w_ref.shape[0] :], w_rest_ref, sem)
    fetch_w.start()
    kv_width = other_ref.shape[1] // 2
    blocks = other_ref.shape[0] // ROWS
    bias = jnp.concatenate(
        [masked_bias(first_ref[i], start_ref, first_ref[blocks]) for i in range(blocks)], axis=1
    )
    for pair in range(kv_width // HEAD_DIM):
        low, high = pair * HEAD_DIM, (pair + 1) * HEAD_DIM
        scores = biased_scores(q_ref, other_ref[:, low:high], bias, pair)
        rows = slice(pair * GROUP * ROWS, (pair + 1) * GROUP * ROWS)
        old_peak = peak_ref[rows, :]
        peak = jnp.maximum(old_peak, jnp.max(scores, axis=1, keepdims=True))
        weights = jnp.exp2((scores - peak[:, :1]) * EXP_SCALE)
        keep = jnp.exp2((old_peak - peak) * EXP_SCALE)
        total = total_ref[rows, :] * keep + jnp.sum(weights, axis=1, keepdims=True)
        mixed = mixed_ref[rows, :] * keep + jnp.dot(
            weights.astype(jnp.bfloat16),
            other_ref[:, kv_width + low : kv_width + high],
            preferred_element_type=jnp.float32,
        )
        mixed = (mixed / total).astype(jnp.bfloat16)
        for h in range(GROUP):
            at = (pair * GROUP + h) * HEAD_DIM
            attended_ref[:, at : at + HEAD_DIM] = mixed[h * ROWS : (h + 1) * ROWS]
    fetch_w.wait()
    for i, out in enumerate(outs):
        part = project(attended_ref[...], (w_ref, w_rest_ref), first_ref[blocks + 1 + i])
        out[...] = part.astype(out.dtype)


def vmem(count):
    return [pl.BlockSpec(memory_space=pltpu.VMEM)] * count


def join_kernel(*refs):
    blocks, (first_ref, out_ref, first_out) = refs[:-3], refs[-3:]
    for i, block in enumerate(blocks):
        out_ref[i * ROWS : (i + 1) * ROWS, :] = block[...]
    first_out[...] = first_ref[...]


def join(blocks, cross):
    shape = (len(blocks) * ROWS, blocks[0].shape[1])
    return pl.pallas_call(
        join_kernel,
        out_shape=(
            jax.ShapeDtypeStruct(shape, blocks[0].dtype),
            jax.ShapeDtypeStruct(cross.shape, cross.dtype),
        ),
        in_specs=vmem(len(blocks) + 1),
        out_specs=tuple(vmem(2)),
        compiler_params=pltpu.CompilerParams(vmem_limit_bytes=4 * 2**20),
        name="join",
    )(*blocks, cross)


def half_weight(out_weight):
    rows, columns = out_weight.shape
    return jax.ShapeDtypeStruct((rows // 2, columns), out_weight.dtype)


def attend_local(firsts, doc_lengths, queries, out_weight, blocks):
    rows = queries.shape[0] * queries.shape[1] // HEAD_DIM
    state = jax.ShapeDtypeStruct((rows, HEAD_DIM), jnp.float32)
    keys = ROWS * len(blocks)
    return pl.pallas_call(
        local_kernel,
        out_shape=(state,) * 3
        + (
            jax.ShapeDtypeStruct((ROWS, ROWS), jnp.int32),
            jax.ShapeDtypeStruct(queries.shape, queries.dtype),
            half_weight(out_weight),
        ),
        in_specs=[pl.BlockSpec(memory_space=pltpu.SMEM)] * 2
        + [pl.BlockSpec(memory_space=pltpu.HBM)] * 2
        + vmem(len(blocks)),
        out_specs=tuple(vmem(6)),
        scratch_shapes=[pltpu.SemaphoreType.DMA((2,))],
        compiler_params=pltpu.CompilerParams(vmem_limit_bytes=16 * 2**20),
        cost_estimate=pl.CostEstimate(
            flops=4 * rows * keys * HEAD_DIM,
            bytes_accessed=4 * rows * keys,
            transcendentals=rows * keys,
        ),
        name="attend_local",
    )(firsts, doc_lengths, queries, out_weight, *blocks)


def attend_rest(firsts, out_weight, other, state, width):
    queries = state[-2]
    rows = queries.shape[0] * queries.shape[1] // HEAD_DIM
    keys = other.shape[0]
    half = half_weight(out_weight)
    kinds = (jnp.bfloat16, jnp.bfloat16, jnp.float32, jnp.float32)
    return pl.pallas_call(
        rest_kernel,
        out_shape=tuple(jax.ShapeDtypeStruct((queries.shape[0], width), k) for k in kinds),
        in_specs=[
            pl.BlockSpec(memory_space=pltpu.SMEM),
            pl.BlockSpec(memory_space=pltpu.HBM),
        ]
        + vmem(1 + len(state)),
        out_specs=tuple(vmem(4)),
        scratch_shapes=[
            pltpu.VMEM(queries.shape, jnp.bfloat16),
            pltpu.VMEM(half.shape, half.dtype),
            pltpu.SemaphoreType.DMA,
        ],
        compiler_params=pltpu.CompilerParams(vmem_limit_bytes=20 * 2**20),
        cost_estimate=pl.CostEstimate(
            flops=4 * rows * keys * HEAD_DIM + 8 * queries.size * width,
            bytes_accessed=4 * rows * keys + out_weight.size,
            transcendentals=rows * keys,
        ),
        name="attend_rest",
    )(firsts, out_weight, other, *state)


def layer(queries, key_rows, values, doc_lengths, out_weight):
    my_index = lax.axis_index("ctx")
    head = lax.axis_index("head")
    heads = lax.axis_size("head")
    chips = lax.axis_size("ctx") // 2
    chip, core = my_index // 2, my_index % 2

    kv_width = key_rows.shape[1]
    zero = jnp.zeros((), key_rows.dtype)
    own = lax.pad(key_rows, zero, ((0, 0, 0), (0, kv_width, 0))) + lax.pad(
        values, zero, ((0, 0, 0), (kv_width, 0, 0))
    )
    own = lax.optimization_barrier(own)
    back, cross = gather_blocks(own)
    blocks = [back[i] for i in range(BACK, 0, -1)] + [own]
    joined, cross = join(blocks, cross)
    blocks = blocks + [cross]
    other = lax.ppermute(joined, "ctx", [(i, i ^ 1) for i in range(2 * chips)])

    query_first = my_index * ROWS
    ahead = jnp.arange(BACK + 1, dtype=jnp.int32) - BACK + chip
    cross_first = jnp.where(core == 0, 2 * ROWS * (chip - 8) + ROWS, -ROWS)
    local_first = jnp.concatenate(
        [2 * ROWS * ahead + ROWS * core, jnp.stack([cross_first, query_first])]
    )
    doc_lengths = pltpu.with_memory_space_constraint(doc_lengths, pltpu.HBM)
    queries = pltpu.with_memory_space_constraint(queries, pltpu.HBM)
    out_weight = pltpu.with_memory_space_constraint(out_weight, pltpu.HBM)
    near, across = head ^ 1, heads - 1 - head
    first_mate = jnp.where(core == 0, near, across)
    second_mate = jnp.where(core == 0, across, near)
    rest_first = jnp.concatenate(
        [2 * ROWS * ahead + ROWS * (1 - core), jnp.stack([query_first, head ^ 2, first_mate, second_mate, head])]
    )
    width = out_weight.shape[1] // heads

    state = attend_local(local_first, doc_lengths, queries, out_weight, blocks)
    far_part, mate_part, second_part, own_part = attend_rest(
        rest_first, out_weight, other, state, width
    )
    far_got = head_swap(far_part, 0)
    mate_got = head_swap(mate_part, 0)
    passed = (second_part + far_got.astype(jnp.float32)).astype(jnp.bfloat16)
    last_got = head_swap(passed, 1)
    return (own_part + mate_got.astype(jnp.float32) + last_got.astype(jnp.float32)).astype(
        jnp.bfloat16
    )


def solution(mesh):
    return jax.shard_map(
        layer,
        mesh=mesh,
        in_specs=(
            P(("batch", "ctx"), "head"),
            P(("batch", "ctx"), "head"),
            P(("batch", "ctx"), "head"),
            P("batch"),
            P("head", None),
        ),
        out_specs=P(("batch", "ctx"), "head"),
        check_vma=False,
    )
```

```python
import math

import jax
import jax.numpy as jnp
from jax import lax
from jax.experimental import pallas as pl
from jax.experimental.pallas import tpu as pltpu
from jax.sharding import PartitionSpec as P


HEADS = 32
KV_HEADS = 8
HEAD_DIM = 128
GROUP = HEADS // KV_HEADS
ROWS = 128
FAR = 1e30
BACK = 7
EXP_SCALE = HEAD_DIM ** (-0.5) * math.log2(math.e)


def chip_send(value, chips, targets):
    pairs = []
    for target in targets:
        if 0 <= target - chips < lax.axis_size("ctx") // 2:
            pairs += [(2 * (target - chips) + core, 2 * target + core) for core in range(2)]
    return lax.ppermute(value, "ctx", pairs)


def gather_blocks(own):
    chips = lax.axis_size("ctx") // 2
    back = {}
    back[1] = chip_send(own, 1, range(1, chips))
    cross = lax.ppermute(own, "ctx", [(2 * c - 15, 2 * c) for c in range(8, chips)])
    back[7] = chip_send(own, 7, range(7, chips))
    back[2] = chip_send(back[1], 1, range(2, chips))
    relayed = chip_send(back[7], -1, range(6, chips - 1))
    back[6] = relayed + chip_send(own, 6, range(chips - 1, chips))
    back[3] = chip_send(back[2], 1, range(3, chips))
    back[4] = chip_send(back[2], 2, range(4, chips))
    relayed = chip_send(back[6], -1, range(5, chips - 2))
    back[5] = relayed + chip_send(own, 5, range(chips - 2, chips))
    return back, cross


def head_swap(value, stage):
    heads = lax.axis_size("head")
    pairs = []
    for index in range(lax.axis_size("ctx")):
        for head in range(heads):
            partner = head ^ 1 if (stage + index) % 2 == 0 else heads - 1 - head
            pairs.append((index * heads + head, index * heads + partner))
    return lax.ppermute(value, ("ctx", "head"), pairs)


def masked_bias(first, start_ref, query_first):
    lane = lax.broadcasted_iota(jnp.int32, (ROWS, ROWS), 1)
    row = lax.broadcasted_iota(jnp.int32, (ROWS, ROWS), 0)
    key_pos = lane + first
    keep = (key_pos >= start_ref[...]) & (key_pos <= row + query_first)
    return jnp.where(keep, 0.0, -FAR).astype(jnp.float32)


def stacked_queries(q_ref, pair):
    return jnp.concatenate(
        [
            q_ref[:, (pair * GROUP + h) * HEAD_DIM : (pair * GROUP + h + 1) * HEAD_DIM]
            for h in range(GROUP)
        ],
        axis=0,
    )


def biased_scores(q_ref, keys, bias, pair):
    scores = lax.dot_general(
        stacked_queries(q_ref, pair),
        keys,
        (((1,), (1,)), ((), ())),
        preferred_element_type=jnp.float32,
    )
    count = keys.shape[0]
    return (scores.reshape(GROUP, ROWS, count) + bias[None]).reshape(GROUP * ROWS, count)


def document_starts(length_ref, query_first):
    query_pos = lax.broadcasted_iota(jnp.int32, (8, ROWS), 1) + query_first
    starts = jnp.zeros_like(query_pos)
    end = jnp.int32(0)
    for i in range(length_ref.shape[0]):
        end = end + length_ref[i]
        starts = jnp.where(query_pos >= end, end, starts)
    return jnp.broadcast_to(starts[:1], (ROWS, ROWS)).T


def local_kernel(first_ref, length_ref, w_hbm, q_ref, *refs):
    blocks, (peak_ref, total_ref, mixed_ref, start_ref, w_ref, sem) = refs[:-6], refs[-6:]
    fetch_w = pltpu.make_async_copy(w_hbm.at[: w_ref.shape[0]], w_ref, sem)
    fetch_w.start()
    start_ref[...] = document_starts(length_ref, first_ref[len(blocks)])
    kv_width = blocks[0].shape[1] // 2
    bias = jnp.concatenate(
        [masked_bias(first_ref[i], start_ref, first_ref[len(blocks)]) for i in range(len(blocks))],
        axis=1,
    )
    for pair in range(kv_width // HEAD_DIM):
        low, high = pair * HEAD_DIM, (pair + 1) * HEAD_DIM
        keys = jnp.concatenate([b[:, low:high] for b in blocks], axis=0)
        vals = jnp.concatenate([b[:, kv_width + low : kv_width + high] for b in blocks], axis=0)
        scores = biased_scores(q_ref, keys, bias, pair)
        peak = jnp.max(scores, axis=1, keepdims=True)
        weights = jnp.exp2((scores - peak) * EXP_SCALE)
        rows = slice(pair * GROUP * ROWS, (pair + 1) * GROUP * ROWS)
        wide = (GROUP * ROWS, HEAD_DIM)
        peak_ref[rows, :] = jnp.broadcast_to(peak, wide)
        total_ref[rows, :] = jnp.broadcast_to(jnp.sum(weights, axis=1, keepdims=True), wide)
        mixed_ref[rows, :] = jnp.dot(
            weights.astype(jnp.bfloat16), vals, preferred_element_type=jnp.float32
        )
    fetch_w.wait()


def project(attended, weights, column):
    rows, width = weights[0].shape[0], ROWS * GROUP * 2
    at = pl.multiple_of(column * width, width)
    return sum(
        jnp.dot(
            attended[:, i * rows : (i + 1) * rows],
            half[:, pl.ds(at, width)],
            preferred_element_type=jnp.float32,
        )
        for i, half in enumerate(weights)
    )


def rest_kernel(
    first_ref,
    w_hbm,
    other_ref,
    peak_ref,
    total_ref,
    mixed_ref,
    start_ref,
    q_ref,
    w_ref,
    *refs,
):
    outs, (attended_ref, w_rest_ref, sem) = refs[:-3], refs[-3:]
    fetch_w = pltpu.make_async_copy(w_hbm.at[w_ref.shape[0] :], w_rest_ref, sem)
    fetch_w.start()
    kv_width = other_ref.shape[1] // 2
    blocks = other_ref.shape[0] // ROWS
    bias = jnp.concatenate(
        [masked_bias(first_ref[i], start_ref, first_ref[blocks]) for i in range(blocks)], axis=1
    )
    for pair in range(kv_width // HEAD_DIM):
        low, high = pair * HEAD_DIM, (pair + 1) * HEAD_DIM
        scores = biased_scores(q_ref, other_ref[:, low:high], bias, pair)
        rows = slice(pair * GROUP * ROWS, (pair + 1) * GROUP * ROWS)
        old_peak = peak_ref[rows, :]
        peak = jnp.maximum(old_peak, jnp.max(scores, axis=1, keepdims=True))
        weights = jnp.exp2((scores - peak[:, :1]) * EXP_SCALE)
        keep = jnp.exp2((old_peak - peak) * EXP_SCALE)
        total = total_ref[rows, :] * keep + jnp.sum(weights, axis=1, keepdims=True)
        mixed = mixed_ref[rows, :] * keep + jnp.dot(
            weights.astype(jnp.bfloat16),
            other_ref[:, kv_width + low : kv_width + high],
            preferred_element_type=jnp.float32,
        )
        mixed = (mixed / total).astype(jnp.bfloat16)
        for h in range(GROUP):
            at = (pair * GROUP + h) * HEAD_DIM
            attended_ref[:, at : at + HEAD_DIM] = mixed[h * ROWS : (h + 1) * ROWS]
    fetch_w.wait()
    for i, out in enumerate(outs):
        part = project(attended_ref[...], (w_ref, w_rest_ref), first_ref[blocks + 1 + i])
        out[...] = part.astype(out.dtype)


def vmem(count):
    return [pl.BlockSpec(memory_space=pltpu.VMEM)] * count


def join_kernel(*refs):
    blocks, (first_ref, out_ref, first_out) = refs[:-3], refs[-3:]
    for i, block in enumerate(blocks):
        out_ref[i * ROWS : (i + 1) * ROWS, :] = block[...]
    first_out[...] = first_ref[...]


def join(blocks, cross):
    shape = (len(blocks) * ROWS, blocks[0].shape[1])
    return pl.pallas_call(
        join_kernel,
        out_shape=(
            jax.ShapeDtypeStruct(shape, blocks[0].dtype),
            jax.ShapeDtypeStruct(cross.shape, cross.dtype),
        ),
        in_specs=vmem(len(blocks) + 1),
        out_specs=tuple(vmem(2)),
        compiler_params=pltpu.CompilerParams(vmem_limit_bytes=4 * 2**20),
        name="join",
    )(*blocks, cross)


def half_weight(out_weight):
    rows, columns = out_weight.shape
    return jax.ShapeDtypeStruct((rows // 2, columns), out_weight.dtype)


def attend_local(firsts, doc_lengths, queries, out_weight, blocks):
    rows = queries.shape[0] * queries.shape[1] // HEAD_DIM
    state = jax.ShapeDtypeStruct((rows, HEAD_DIM), jnp.float32)
    keys = ROWS * len(blocks)
    return pl.pallas_call(
        local_kernel,
        out_shape=(state,) * 3
        + (
            jax.ShapeDtypeStruct((ROWS, ROWS), jnp.int32),
            half_weight(out_weight),
        ),
        in_specs=[pl.BlockSpec(memory_space=pltpu.SMEM)] * 2
        + [pl.BlockSpec(memory_space=pltpu.HBM)]
        + vmem(1 + len(blocks)),
        out_specs=tuple(vmem(5)),
        scratch_shapes=[pltpu.SemaphoreType.DMA],
        compiler_params=pltpu.CompilerParams(vmem_limit_bytes=16 * 2**20),
        cost_estimate=pl.CostEstimate(
            flops=4 * rows * keys * HEAD_DIM,
            bytes_accessed=4 * rows * keys,
            transcendentals=rows * keys,
        ),
        name="attend_local",
    )(firsts, doc_lengths, out_weight, queries, *blocks)


def attend_rest(firsts, out_weight, other, state, width):
    queries = state[-2]
    rows = queries.shape[0] * queries.shape[1] // HEAD_DIM
    keys = other.shape[0]
    half = half_weight(out_weight)
    kinds = (jnp.bfloat16, jnp.bfloat16, jnp.float32, jnp.float32)
    return pl.pallas_call(
        rest_kernel,
        out_shape=tuple(jax.ShapeDtypeStruct((queries.shape[0], width), k) for k in kinds),
        in_specs=[
            pl.BlockSpec(memory_space=pltpu.SMEM),
            pl.BlockSpec(memory_space=pltpu.HBM),
        ]
        + vmem(1 + len(state)),
        out_specs=tuple(vmem(4)),
        scratch_shapes=[
            pltpu.VMEM(queries.shape, jnp.bfloat16),
            pltpu.VMEM(half.shape, half.dtype),
            pltpu.SemaphoreType.DMA,
        ],
        compiler_params=pltpu.CompilerParams(vmem_limit_bytes=20 * 2**20),
        cost_estimate=pl.CostEstimate(
            flops=4 * rows * keys * HEAD_DIM + 8 * queries.size * width,
            bytes_accessed=4 * rows * keys + out_weight.size,
            transcendentals=rows * keys,
        ),
        name="attend_rest",
    )(firsts, out_weight, other, *state)


def layer(queries, key_rows, values, doc_lengths, out_weight):
    my_index = lax.axis_index("ctx")
    head = lax.axis_index("head")
    heads = lax.axis_size("head")
    chips = lax.axis_size("ctx") // 2
    chip, core = my_index // 2, my_index % 2

    kv_width = key_rows.shape[1]
    zero = jnp.zeros((), key_rows.dtype)
    own = lax.pad(key_rows, zero, ((0, 0, 0), (0, kv_width, 0))) + lax.pad(
        values, zero, ((0, 0, 0), (kv_width, 0, 0))
    )
    own = lax.optimization_barrier(own)
    back, cross = gather_blocks(own)
    blocks = [back[i] for i in range(BACK, 0, -1)] + [own]
    joined, cross = join(blocks, cross)
    blocks = blocks + [cross]
    other = lax.ppermute(joined, "ctx", [(i, i ^ 1) for i in range(2 * chips)])

    query_first = my_index * ROWS
    ahead = jnp.arange(BACK + 1, dtype=jnp.int32) - BACK + chip
    cross_first = jnp.where(core == 0, 2 * ROWS * (chip - 8) + ROWS, -ROWS)
    local_first = jnp.concatenate(
        [2 * ROWS * ahead + ROWS * core, jnp.stack([cross_first, query_first])]
    )
    doc_lengths = pltpu.with_memory_space_constraint(doc_lengths, pltpu.HBM)
    queries = queries * (my_index >= 0).astype(queries.dtype)
    out_weight = pltpu.with_memory_space_constraint(out_weight, pltpu.HBM)
    near, across = head ^ 1, heads - 1 - head
    first_mate = jnp.where(core == 0, near, across)
    second_mate = jnp.where(core == 0, across, near)
    rest_first = jnp.concatenate(
        [2 * ROWS * ahead + ROWS * (1 - core), jnp.stack([query_first, head ^ 2, first_mate, second_mate, head])]
    )
    width = out_weight.shape[1] // heads

    *state, half = attend_local(local_first, doc_lengths, queries, out_weight, blocks)
    state = (*state, queries, half)
    far_part, mate_part, second_part, own_part = attend_rest(
        rest_first, out_weight, other, state, width
    )
    far_got = head_swap(far_part, 0)
    mate_got = head_swap(mate_part, 0)
    passed = (second_part + far_got.astype(jnp.float32)).astype(jnp.bfloat16)
    last_got = head_swap(passed, 1)
    return (own_part + mate_got.astype(jnp.float32) + last_got.astype(jnp.float32)).astype(
        jnp.bfloat16
    )


def solution(mesh):
    return jax.shard_map(
        layer,
        mesh=mesh,
        in_specs=(
            P(("batch", "ctx"), "head"),
            P(("batch", "ctx"), "head"),
            P(("batch", "ctx"), "head"),
            P("batch"),
            P("head", None),
        ),
        out_specs=P(("batch", "ctx"), "head"),
        check_vma=False,
    )
```
